256 devices in a mesh: dp: 32 (over y, x, z_lo), mp: 8 (over z_hi, core).
Axes of the slice: x: 4, y: 4, z: 8 (z_hi: 4, z_lo: 2; z = z_hi * 2 + z_lo), core: 2. Of those that a mesh axis runs over, the one named last changes fastest.
Arguments:
- query: bfloat16 [2048, 4096], P('dp', 'mp'), may hold values from -144 to 144
- new_key: bfloat16 [2048, 4096], P('dp', 'mp'), may hold values from -6 to 6
- new_value: bfloat16 [2048, 4096], P('dp', 'mp'), may hold values from -6 to 6
- cache_key: bfloat16 [2048, 32, 16, 128], P('dp', 'mp'), may hold values from -6 to 6
- cache_value: bfloat16 [2048, 32, 16, 128], P('dp', 'mp'), may hold values from -6 to 6
- cache_len: int32 [2048], P('dp'), may hold values from 2 to 16
- residual: bfloat16 [2048, 8192], P('dp'), may hold values from -6 to 6
- out_weight: bfloat16 [4096, 8192], P('mp'), may hold values from -0.1875 to 0.1875
- norm_gain: bfloat16 [8192], P('mp'), may hold values from 0.25 to 1.75
- codec_weight: bfloat16 [8192, 1024], P('mp'), may hold values from -0.125 to 0.125
- finished: int32 [2048], P('dp'), may hold values from 0 to 1
- owner: int32 [2048], P('dp'), may hold values from 0 to 31, as said below
- frames: bfloat16 [32768, 1024], P('dp', 'mp'), may hold values from -6 to 6
- snake_alpha: float32 [1024], P('mp'), may hold values from 0.5 to 2
- filter_weight: bfloat16 [7, 1024, 1024], P(None, None, 'mp'), may hold values from -0.125 to 0.125
- conv_bias: float32 [1024], P('mp'), may hold values from -4 to 4
Outputs:
- hidden: bfloat16 [2048, 8192], P('dp', 'mp')
- audio: bfloat16 [32768, 1024], P('dp', 'mp')
The draws below stay inside these ranges and needn't reach their ends.
Inputs may be any that keep to these rules, and one draw needn't show every extreme that they name: Within each aligned block of 64 rows, at most 4 finished rows name the same owner, and some owner is named by exactly 4 finished rows of the block.
All inputs are finite; a program needn't handle non-finite values.
Results may differ from the reference program's by a relative error of at most 0.0056.
Values may be sent and summed in bfloat16 or wider, within the bound.
No kernel may reach another device: no remote copies, remote signals or barrier semaphores. Data moves between devices by JAX's collectives and lax.ppermute only.
A program may use at most 128 MiB of HBM per device.

```python
import math
import jax
import jax.numpy as jnp
from jax import lax

D = 8192
HEADS = 32
HD = 128
CODEC = 1024
ROW_DEV = 64
CACHE = 16
FRAMES = 1024
KERNEL_TAPS = 7
DILATION_STEP = 3
CAP = 4
ROWS = 2048
TOTAL_FRAMES = 32768
N_DP = 32


def key_tables(key):
    base = jax.random.fold_in(key, 11)
    first, second = jax.random.split(base, 2)
    keys = jnp.clip(jax.random.normal(first, (ROWS, HEADS, CACHE, HD), jnp.float32), -6.0, 6.0)
    queries = jnp.clip(jax.random.normal(second, (ROWS, HEADS, HD), jnp.float32), -6.0, 6.0)
    return (keys, queries.reshape(ROWS, HEADS * HD))


def draw_query(key, part):
    return key_tables(key)[1].astype(jnp.bfloat16)


def draw_cache_key(key, part):
    return key_tables(key)[0].astype(jnp.bfloat16)


def route_tables(key):
    base = jax.random.fold_in(key, 23)
    first, second, third = jax.random.split(base, 3)
    owners_perm = jax.vmap(lambda sub: jax.random.permutation(sub, N_DP))(jax.random.split(first, N_DP))
    orders = jax.vmap(lambda sub: jax.random.permutation(sub, ROW_DEV))(jax.random.split(second, N_DP))
    owners = jnp.take_along_axis(owners_perm, orders // CAP, axis=1)
    coins = (jax.random.randint(third, (N_DP, ROW_DEV), 0, 8) < 7).astype(jnp.int32)
    done = jnp.where(orders < CAP, 1, coins)
    return (owners.reshape(ROWS).astype(jnp.int32), done.reshape(ROWS).astype(jnp.int32))


def draw_owner(key, part):
    return route_tables(key)[0]


def draw_finished(key, part):
    return route_tables(key)[1]


def touch_ends(array, stream_key, smallest, top_value):
    dims = array.shape
    spot = [jax.random.randint(jax.random.fold_in(stream_key, axis), (), 0, dims[axis]) for axis in range(len(dims))]
    array = array.at[tuple(spot)].set(smallest)
    longest = dims.index(max(dims))
    spot[longest] = (spot[longest] + 1) % dims[longest]
    return array.at[tuple(spot)].set(top_value)


def steps_of(rng, dims, shards, smallest, high):
    factor_of, own = 1.0, jax.random.fold_in(rng, 6)
    for dim, shards_of in shards:
        heights = jnp.exp(jax.random.uniform(jax.random.fold_in(own, dim), (shards_of,), jnp.float32, smallest / len(shards), high / len(shards)))
        factor_of = factor_of * jnp.repeat(heights, dims[dim] // shards_of).reshape([-1 if axis == dim else 1 for axis in range(len(dims))])
    return factor_of


def noise(own_key, shape, width, reach, cuts=(), held_as=jnp.bfloat16):
    loudness = steps_of(own_key, shape, cuts, -0.22, 0.18) if cuts else 1.0
    result = jax.random.normal(own_key, shape, jnp.float32) * width * loudness
    return jnp.minimum(jnp.maximum(result, -reach), reach).astype(held_as)


def setup_inputs(seed: int = 0) -> dict:
    arg_keys = jax.random.split(jax.random.key(seed), 17)
    query = draw_query(jax.random.fold_in(arg_keys[16], 71), 0)
    new_key = noise(arg_keys[1], (ROWS, HEADS * HD), 1.0, 6.0, ((0, 32), (1, 8)))
    new_value = noise(arg_keys[2], (ROWS, HEADS * HD), 1.0, 6.0, ((0, 32), (1, 8)))
    cache_key = draw_cache_key(jax.random.fold_in(arg_keys[16], 71), 0)
    cache_value = noise(arg_keys[4], (ROWS, HEADS, CACHE, HD), 1.0, 6.0, ((0, 32), (1, 8)))
    cache_len = touch_ends(jax.random.randint(arg_keys[5], (ROWS,), 2, CACHE + 1), jax.random.fold_in(arg_keys[5], 1), 2, CACHE).astype(jnp.int32)
    residual = noise(arg_keys[6], (ROWS, D), 1.0, 6.0, ((0, 32),))
    out_weight = noise(arg_keys[7], (HEADS * HD, D), (HEADS * HD // 4) ** -0.5, 0.1875, ((0, 8),))
    norm_gain = jnp.clip(1.0 + 0.15 * jax.random.normal(arg_keys[8], (D,), jnp.float32), 0.25, 1.75).astype(jnp.bfloat16)
    codec_weight = noise(arg_keys[9], (D, CODEC), (D // 4) ** -0.5, 0.125, ((0, 8),))
    finished = draw_finished(jax.random.fold_in(arg_keys[16], 71), 0)
    owner = draw_owner(jax.random.fold_in(arg_keys[16], 71), 0)
    frames = noise(arg_keys[12], (TOTAL_FRAMES, CODEC), 1.0, 6.0, ((0, 32), (1, 8)))
    snake_alpha = jnp.clip(jnp.exp(math.log(2.0) - 1.3862944 * jax.random.uniform(arg_keys[13], (CODEC,), jnp.float32) ** steps_of(arg_keys[13], (CODEC,), ((0, 8),), -0.2, 0.2)), 0.5, 2.0)
    filter_weight = noise(arg_keys[14], (KERNEL_TAPS, CODEC, CODEC), (KERNEL_TAPS * CODEC // 4) ** -0.5, 0.125, ((2, 8),))
    conv_bias = noise(arg_keys[15], (CODEC,), 1.0, 4.0, ((0, 8),), jnp.float32)
    return dict(query=query, new_key=new_key, new_value=new_value, cache_key=cache_key, cache_value=cache_value, cache_len=cache_len, residual=residual, out_weight=out_weight, norm_gain=norm_gain, codec_weight=codec_weight, finished=finished, owner=owner, frames=frames, snake_alpha=snake_alpha, filter_weight=filter_weight, conv_bias=conv_bias)


def reference(query, new_key, new_value, cache_key, cache_value, cache_len, residual, out_weight, norm_gain, codec_weight, finished, owner, frames, snake_alpha, filter_weight, conv_bias):
    count = query.shape[0]
    heads = cache_key.shape[1]
    depth = cache_key.shape[3]
    positions = cache_key.shape[2]
    scale = 1.0 / jnp.sqrt(jnp.float32(depth))
    queries = query.reshape(count, heads, depth).astype(jnp.float32)
    fresh_key = new_key.reshape(count, heads, depth).astype(jnp.float32)
    fresh_value = new_value.reshape(count, heads, depth).astype(jnp.float32)
    scores = jnp.einsum('rhd,rhld->rhl', queries, cache_key.astype(jnp.float32)) * scale
    own_score = jnp.einsum('rhd,rhd->rh', queries, fresh_key) * scale
    valid = jnp.arange(positions, dtype=jnp.int32)[None, :] < cache_len[:, None]
    scores = jnp.where(valid[:, None, :], scores, -1e+30)
    top = jnp.maximum(lax.optimization_barrier(jnp.max(scores, axis=-1)), own_score)
    expo = jnp.where(valid[:, None, :], jnp.exp(scores - top[..., None]), 0.0)
    own_expo = jnp.exp(own_score - top)
    total = lax.optimization_barrier(jnp.sum(expo, axis=-1)) + own_expo
    weights = (expo / total[..., None]).astype(jnp.bfloat16)
    own_weight = (own_expo / total).astype(jnp.bfloat16)
    attended = jnp.einsum('rhl,rhld->rhd', weights.astype(jnp.float32), cache_value.astype(jnp.float32))
    attended = attended + own_weight.astype(jnp.float32)[..., None] * fresh_value
    attended = attended.astype(jnp.bfloat16).reshape(count, heads * depth)
    projected = jnp.dot(attended, out_weight, preferred_element_type=jnp.float32)
    hidden = (residual.astype(jnp.float32) + projected).astype(jnp.bfloat16)
    wide = hidden.astype(jnp.float32)
    meansq = lax.optimization_barrier(jnp.mean(wide * wide, axis=-1))
    normed = (wide * norm_gain.astype(jnp.float32)).astype(jnp.bfloat16)
    latent = jnp.dot(normed, codec_weight, preferred_element_type=jnp.float32) * lax.rsqrt(meansq + 1e-05)[:, None]
    latent = latent.astype(jnp.bfloat16)
    index = jnp.arange(count, dtype=jnp.int32)
    block = index // ROW_DEV
    earlier = (block[:, None] == block[None, :]) & (owner[:, None] == owner[None, :]) & (finished[None, :] == 1) & (index[None, :] < index[:, None])
    slot = lax.optimization_barrier(jnp.sum(earlier.astype(jnp.int32), axis=1)).astype(jnp.int32)
    overall_frames = frames.shape[0]
    target = (owner * FRAMES + block * CAP + slot).astype(jnp.int32)
    target = jnp.where(finished == 1, target, overall_frames).astype(jnp.int32)
    added = jnp.zeros(frames.shape, jnp.float32).at[target].add(latent.astype(jnp.float32), mode='drop')
    mix = frames.astype(jnp.float32) + added
    alpha = snake_alpha.astype(jnp.float32)
    act = (mix + jnp.sin(alpha * mix) ** 2 / alpha).astype(jnp.bfloat16)
    filter_span = KERNEL_TAPS // 2 * DILATION_STEP
    padded_frames = jnp.pad(act, ((filter_span, filter_span), (0, 0)))
    dilated_filter = jnp.zeros(mix.shape, jnp.float32)
    for tap_index in range(KERNEL_TAPS):
        dilated_filter = dilated_filter + jnp.dot(padded_frames[tap_index * DILATION_STEP:tap_index * DILATION_STEP + overall_frames], filter_weight[tap_index], preferred_element_type=jnp.float32)
    audio = (mix + conv_bias.astype(jnp.float32) + dilated_filter).astype(jnp.bfloat16)
    return (hidden, audio)
```

```python
import math
import jax
import jax.numpy as jnp
from jax import lax
from jax.experimental import pallas as pl
from jax.experimental.pallas import tpu as pltpu
from jax.sharding import Mesh
from jax.sharding import PartitionSpec as P

TAPS = 7
STEP = 3
CAP = 4
ZH = 4
MP = ("zh", "c")
F32 = jnp.float32
BF16 = jnp.bfloat16
ORDER = (2, 1, 3, 0)
VM = pl.BlockSpec(memory_space=pltpu.VMEM)
ANY = pl.BlockSpec(memory_space=pl.ANY)
DMA = pltpu.SemaphoreType.DMA


def params(mib=8):
    return pltpu.CompilerParams(vmem_limit_bytes=mib * 1024 * 1024)


def sds(shape, dtype):
    return jax.ShapeDtypeStruct(shape, dtype)


def placed_in(x, space):
    return pltpu.with_memory_space_constraint(x, space)


def call(kernel, name, outs, ins, scratch=(), far=(), far_outs=(), mib=8, alias=None, cost=None):
    return pl.pallas_call(
        kernel,
        in_specs=[ANY if i in far else VM for i in range(len(ins))],
        out_specs=[ANY if i in far_outs else VM for i in range(len(outs))] if isinstance(outs, list) else ANY if far_outs else VM,
        out_shape=outs,
        scratch_shapes=list(scratch),
        input_output_aliases=alias or {},
        compiler_params=params(mib),
        cost_estimate=cost,
        name=name,
    )(*[placed_in(x, pltpu.HBM if i in far else pltpu.VMEM) for i, x in enumerate(ins)])


def work(us):
    return pl.CostEstimate(flops=int(us * 1e7), transcendentals=0, bytes_accessed=int(us * 3e4))


def iota(shape, dim):
    return lax.broadcasted_iota(jnp.int32, shape, dim)


def as_column(row, size):
    diag = iota((size, size), 0) == iota((size, size), 1)
    return jnp.sum(jnp.where(diag, jnp.broadcast_to(row, (size, size)), 0), axis=1, keepdims=True)


def sin_squared(x):
    k = jnp.floor(x * (1.0 / math.pi) + 0.5)
    r = x - k * 3.140625
    r = r - k * 9.67502593994140625e-4
    r = r - k * 1.509957990978376432e-7
    s = r * r
    p = -1.0 / 39916800.0
    p = p * s + 1.0 / 362880.0
    p = p * s - 1.0 / 5040.0
    p = p * s + 1.0 / 120.0
    p = p * s - 1.0 / 6.0
    y = r + r * (s * p)
    return y * y


def attend_kernel(
    q_hbm, nk_hbm, nv_hbm, ck_hbm, cv_hbm, len_hbm, fin_hbm, own_hbm, w_hbm,
    theirs_ref, att_ref, weight_ref, tgt_ref,
    q_ref, nk_ref, nv_ref, ck_ref, cv_ref, len_ref, fin_ref, own_ref, peer_ref, small_sem, key_sem, value_sem, peer_sem, own_sem,
):
    rows, heads, places, depth = ck_ref.shape
    group = 16
    groups = rows // group
    wide = group * places
    width = weight_ref.shape[2]
    chip, core = lax.axis_index("zh"), lax.axis_index("c")
    small = [
        pltpu.make_async_copy(src, dst, small_sem.at[i])
        for i, (src, dst) in enumerate(
            [(q_hbm, q_ref), (nk_hbm, nk_ref), (nv_hbm, nv_ref), (len_hbm, len_ref), (fin_hbm, fin_ref), (own_hbm, own_ref)]
        )
    ]
    keys, values, theirs, ours = [], [], [], []
    for g in range(groups):
        span = pl.ds(g * group, group)
        keys.append(pltpu.make_async_copy(ck_hbm.at[span], ck_ref.at[span], key_sem.at[g]))
        values.append(pltpu.make_async_copy(cv_hbm.at[span], cv_ref.at[span], value_sem.at[g]))
    for i, d in enumerate(ORDER):
        block = lax.rem(chip + d, ZH) * 2
        for held, to, sem, side in ((theirs, peer_ref, peer_sem, 1 - core), (ours, weight_ref, own_sem, core)):
            at = pl.multiple_of((block + side) * width, width)
            held.append(pltpu.make_async_copy(w_hbm.at[:, pl.ds(at, width)], to.at[i], sem.at[i]))
    for copy in small:
        copy.start()
    for g in range(groups):
        keys[g].start()
        values[g].start()
    for copy in theirs + ours:
        copy.start()
    for copy in small:
        copy.wait()
    scale = 1.0 / math.sqrt(depth)

    fin = fin_ref[...]
    owner = own_ref[...]
    fin_col = as_column(fin, rows)
    owner_col = as_column(owner, rows)
    earlier = (owner_col == owner) & (fin_col == 1) & (iota((rows, rows), 0) < iota((rows, rows), 1))
    slot = jnp.sum(earlier.astype(jnp.int32), axis=0, keepdims=True)
    done = fin == 1
    tgt_ref[0:1] = jnp.where(done, owner * (2 * CAP) + slot, -1)
    tgt_ref[1:2] = jnp.where(done & (owner >= 1), (owner - 1) * (2 * CAP) + CAP + slot, -1)

    length = as_column(len_ref[...], rows)
    offset = iota((group, wide), 1) - places * iota((group, wide), 0)
    for g in range(groups):
        span = slice(g * group, (g + 1) * group)
        inside = (offset >= 0) & (offset < length[span])
        valid = jnp.concatenate([inside.astype(F32)] * heads, axis=0) > 0.5
        keys[g].wait()
        scores, own = [], []
        for h in range(heads):
            cols = slice(h * depth, (h + 1) * depth)
            q = q_ref[span, cols]
            k = ck_ref[span, h].reshape(wide, depth)
            scores.append(lax.dot_general(q, k, (((1,), (1,)), ((), ())), preferred_element_type=F32))
            own.append(jnp.sum(q.astype(F32) * nk_ref[span, cols].astype(F32), axis=1, keepdims=True))
        scores = jnp.where(valid, jnp.concatenate(scores, axis=0) * scale, -1e30)
        own = jnp.concatenate(own, axis=0) * scale
        top = jnp.maximum(jnp.max(scores, axis=1, keepdims=True), own)
        expo = jnp.where(valid, jnp.exp(scores - top), 0.0)
        own_expo = jnp.exp(own - top)
        inv = 1.0 / (jnp.sum(expo, axis=1, keepdims=True) + own_expo)
        weights = (expo * inv).astype(BF16)
        own_weight = (own_expo * inv).astype(BF16).astype(F32)
        values[g].wait()
        for h in range(heads):
            cols = slice(h * depth, (h + 1) * depth)
            part = slice(h * group, (h + 1) * group)
            mixed = jnp.dot(weights[part], cv_ref[span, h].reshape(wide, depth), preferred_element_type=F32)
            att_ref[span, cols] = (mixed + own_weight[part] * nv_ref[span, cols].astype(F32)).astype(BF16)
    att = att_ref[...]
    for i in range(ZH):
        theirs[i].wait()
        theirs_ref[i] = jnp.dot(att, peer_ref[i], preferred_element_type=F32).astype(BF16)
    for copy in ours:
        copy.wait()


def attend(query, new_key, new_value, cache_key, cache_value, cache_len, finished, owner, weight, width):
    rows = query.shape[0]
    depth = weight.shape[0]
    line = lambda x: x.reshape(1, rows)
    ins = (query, new_key, new_value, cache_key, cache_value, line(cache_len), line(finished), line(owner), weight)
    dma = DMA
    return call(
        attend_kernel,
        "attend",
        [
            pltpu.VMEM((ZH, rows, width), BF16),
            pltpu.VMEM((rows, depth), BF16),
            pltpu.VMEM((ZH, depth, width), BF16),
            pltpu.VMEM((2, rows), jnp.int32),
        ],
        ins,
        scratch=[pltpu.VMEM(x.shape, x.dtype) for x in ins[:8]]
        + [pltpu.VMEM((ZH, depth, width), BF16), dma((6,)), dma((rows // 16,)), dma((rows // 16,)), dma((ZH,)), dma((ZH,))],
        far=range(9),
        mib=16,
        cost=work(6),
    )


def project_kernel(att_ref, w_ref, res_hbm, codec_hbm, gain_hbm, out_ref, codec_ref, gain_ref, res_ref, line_ref, sems):
    width = w_ref.shape[2]
    at = pl.multiple_of((lax.axis_index("zh") * 2 + lax.axis_index("c")) * width, width)
    res_copy = pltpu.make_async_copy(res_hbm.at[:, pl.ds(at, width)], res_ref, sems.at[0])
    gain_copy = pltpu.make_async_copy(gain_hbm, line_ref, sems.at[1])
    codec_copy = pltpu.make_async_copy(codec_hbm, codec_ref, sems.at[2])
    res_copy.start()
    gain_copy.start()
    codec_copy.start()
    att = att_ref[...]
    for i, d in enumerate(ORDER):
        part = jnp.dot(att, w_ref[i], preferred_element_type=F32)
        if d == 0:
            res_copy.wait()
            part = part + res_ref[...].astype(F32)
        out_ref[i] = part
    gain_copy.wait()
    gain_ref[...] = line_ref[...].astype(F32).reshape(1, width)
    codec_copy.wait()


def project(attended, weight, residual, codec, gain):
    rows = attended.shape[0]
    count, _, width = weight.shape
    return call(
        project_kernel,
        "project",
        [pltpu.VMEM((count, rows, width), F32), pltpu.VMEM(codec.shape, BF16), pltpu.VMEM((1, width), F32)],
        (attended, weight, residual, codec, gain),
        scratch=[pltpu.VMEM((rows, width), BF16), pltpu.VMEM(gain.shape, BF16), DMA((3,))],
        far=(2, 3, 4),
        cost=work(2),
    )


def pair_kernel(own_ref, peer_ref, *outs):
    for i, out in enumerate(outs):
        out[...] = (own_ref[i] + peer_ref[i].astype(F32)).astype(BF16)


def pair(own, peer):
    _, rows, width = own.shape
    return call(pair_kernel, "pair", [pltpu.VMEM((rows, width), BF16)] * (ZH - 1), (own, peer), cost=work(0.5))


def split_sum(total):
    hi = total.astype(BF16).astype(F32)
    lo = total - hi
    lane = iota((total.shape[0], 128), 1)
    return jnp.where(lane == 0, hi, jnp.where(lane == 1, lo, 0.0)).astype(BF16)


def hidden_kernel(own_ref, peer_ref, r2_ref, r1_ref, r3_ref, gain_ref, codec_ref, hid_ref, keep_ref, send_ref):
    half = codec_ref.shape[1] // 2
    last = ORDER.index(0)
    total = own_ref[last] + peer_ref[last].astype(F32)
    total = total + r2_ref[...].astype(F32) + (r1_ref[...].astype(F32) + r3_ref[...].astype(F32))
    hidden = total.astype(BF16)
    hid_ref[...] = hidden
    wide = hidden.astype(F32)
    normed = (wide * gain_ref[...]).astype(BF16)
    squares = jnp.sum(wide * wide, axis=1, keepdims=True)
    part = jnp.dot(normed, codec_ref[...], preferred_element_type=F32)
    left, right = part[:, :half], part[:, half:]
    first = lax.axis_index("c") == 0
    keep_ref[:, :half] = jnp.where(first, left, right)
    send_ref[:, :half] = jnp.where(first, right, left).astype(BF16)
    keep_ref[:, half:] = jnp.broadcast_to(squares, (squares.shape[0], 128))
    send_ref[:, half:] = split_sum(squares)


def hidden_step(own, peer, r2, r1, r3, gain, codec):
    rows, width = r2.shape
    ext = codec.shape[1] // 2 + 128
    outs = [pltpu.VMEM((rows, width), BF16), pltpu.VMEM((rows, ext), F32), pltpu.VMEM((rows, ext), BF16)]
    return call(hidden_kernel, "hidden", outs, (own, peer, r2, r1, r3, gain, codec), cost=work(2))


def join_kernel(keep_ref, recv_ref, out_ref):
    half = keep_ref.shape[1] - 128
    recv = recv_ref[...].astype(F32)
    out_ref[:, :half] = (keep_ref[:, :half] + recv[:, :half]).astype(BF16)
    squares = keep_ref[:, half : half + 1] + recv[:, half : half + 1] + recv[:, half + 1 : half + 2]
    out_ref[:, half:] = split_sum(squares)


def join(keep, recv):
    return call(join_kernel, "join", pltpu.VMEM(recv.shape, BF16), (keep, recv), cost=work(0.3))


def dispatch_kernel(features, a_ref, b_ref, c_ref, d_ref, tgt_ref, out_ref):
    half = a_ref.shape[1] - 128
    owners, slots, _ = out_ref.shape
    rows = a_ref.shape[0]
    total = (a_ref[...].astype(F32) + b_ref[...].astype(F32)) + (c_ref[...].astype(F32) + d_ref[...].astype(F32))
    squares = total[:, half : half + 1] + total[:, half + 1 : half + 2]
    latent = (total[:, :half] * lax.rsqrt(squares / features + 1e-05)).astype(BF16)
    place = iota((owners * slots, rows), 0)
    onehot = ((place == tgt_ref[0:1]) | (place == tgt_ref[1:2])).astype(F32).astype(BF16)
    placed = jnp.dot(onehot, latent, preferred_element_type=F32)
    out_ref[...] = placed.reshape(owners, slots, half).astype(BF16)


def dispatch(features, owners, parts, targets):
    half = parts[0].shape[1] - 128
    kernel = lambda *refs: dispatch_kernel(features, *refs)
    return call(kernel, "dispatch", pltpu.VMEM((owners, 2 * CAP, half), BF16), (*parts, targets), cost=work(1))


def payload_kernel(frames_hbm, alpha_hbm, out_ref, frames_ref, alpha_ref, sems):
    copies = [
        pltpu.make_async_copy(alpha_hbm, alpha_ref, sems.at[0]),
        pltpu.make_async_copy(frames_hbm, frames_ref, sems.at[1]),
    ]
    for copy in copies:
        copy.start()
    for copy in copies:
        copy.wait()
    count, width = frames_ref.shape
    first = out_ref.shape[0] - count
    raw = frames_ref[...]
    early = 32 * CAP
    alpha = alpha_ref[...]
    mix = raw[early:].astype(F32)
    act = mix + sin_squared(alpha * mix) * (1.0 / alpha)
    out_ref[0:early] = raw[:early]
    out_ref[early:count] = act.astype(BF16)
    hi = alpha.astype(BF16).astype(F32)
    mid = (alpha - hi).astype(BF16).astype(F32)
    lo = alpha - hi - mid
    row = iota((first, width), 0)
    out_ref[count:] = jnp.where(row == 0, hi, jnp.where(row == 1, mid, jnp.where(row == 2, lo, 0.0))).astype(BF16)


def payload(frames, alpha):
    count, width = frames.shape
    return call(
        payload_kernel,
        "payload",
        pltpu.VMEM((count + 16, width), BF16),
        (frames, alpha.reshape(1, width)),
        scratch=[pltpu.VMEM((count, width), BF16), pltpu.VMEM((1, width), F32), DMA((2,))],
        far=(0, 1),
        cost=work(1.5),
    )


HEAD = 32 * CAP
EDGE = 16
TOP = HEAD + EDGE


def taps_sum(y, base, count):
    total = None
    for t in range(TAPS):
        at = base + (t - TAPS // 2) * STEP
        part = y[at : at + count, t * 128 : (t + 1) * 128]
        total = part if total is None else total + part
    return total


CUT = 512


def main_kernel(*refs):
    pieces = refs[:10]
    filt_hbm, own_hbm, bias_hbm, audio_hbm, raw_ref, alpha_ref, near_ref, tail_ref, wcat_ref, ends_ref, bias_ref = refs[10:21]
    act_ref, y_ref, own_ref, out_ref, sems = refs[21:]
    chip, core = lax.axis_index("zh"), lax.axis_index("c")
    copies = [
        pltpu.make_async_copy(filt_hbm.at[t], wcat_ref.at[:, pl.ds(t * 128, 128)], sems.at[t]) for t in range(TAPS)
    ]
    copies.append(pltpu.make_async_copy(own_hbm, own_ref, sems.at[TAPS]))
    copies.append(pltpu.make_async_copy(bias_hbm, bias_ref, sems.at[TAPS + 1]))
    for copy in copies:
        copy.start()
    count = own_ref.shape[0]
    for k in range(8):
        source = lax.rem(chip + k // 2, ZH) * 2 + (core if k % 2 == 0 else 1 - core)
        cols = pl.ds(pl.multiple_of(source * 128, 128), 128)
        if k // 2 == 2:
            head, rest = pieces[4 + k % 2], pieces[6 + k % 2]
            act_ref[0 : CUT - HEAD, cols] = head[HEAD:CUT]
            act_ref[CUT - HEAD :, cols] = rest[0 : count - CUT]
            extra = rest[count - CUT :]
        else:
            head = pieces[k if k < 4 else k + 2]
            act_ref[:, cols] = head[HEAD:count]
            extra = head[count : count + 16]
        raw_ref[:, cols] = head[0:HEAD]
        extra = extra.astype(F32)
        alpha_ref[:, cols] = jnp.broadcast_to(extra[0:1] + extra[1:2] + extra[2:3], (8, 128))
    near_ref[...] = act_ref[0 : 2 * EDGE]
    tail_ref[...] = act_ref[count - HEAD - 2 * EDGE : count - HEAD]
    for copy in copies:
        copy.wait()
    y_ref[...] = jnp.dot(act_ref[...], wcat_ref[...], preferred_element_type=F32)
    inner = count - TOP - EDGE
    conv = taps_sum(y_ref, EDGE, inner)
    mix = own_ref[TOP : TOP + inner].astype(F32)
    out_ref[...] = (mix + bias_ref[...] + conv).astype(BF16)
    ends_ref[0:TOP] = own_ref[0:TOP]
    ends_ref[TOP:] = own_ref[count - EDGE : count]
    last = pltpu.make_async_copy(out_ref, audio_hbm.at[pl.ds(TOP, inner)], sems.at[TAPS + 2])
    last.start()
    last.wait()


def main_conv(pieces, filt, frames, bias):
    count, width = frames.shape
    taps, channels, _ = filt.shape
    outs = [
        pltpu.HBM((count, width), BF16),
        pltpu.VMEM((HEAD, channels), BF16),
        pltpu.VMEM((8, channels), F32),
        pltpu.VMEM((2 * EDGE, channels), BF16),
        pltpu.VMEM((2 * EDGE, channels), BF16),
        pltpu.VMEM((channels, taps * width), BF16),
        pltpu.VMEM((TOP + EDGE, width), BF16),
        pltpu.VMEM((1, width), F32),
    ]
    scratch = [
        pltpu.VMEM((count - HEAD, channels), BF16),
        pltpu.VMEM((count - HEAD, taps * width), F32),
        pltpu.VMEM((count, width), BF16),
        pltpu.VMEM((count - TOP - EDGE, width), BF16),
        DMA((TAPS + 3,)),
    ]
    ins = (*pieces, filt, frames, bias.reshape(1, width))
    return call(main_kernel, "main_conv", outs, ins, scratch, far=(10, 11, 12), far_outs=(0,), mib=16, cost=work(4))


def final_kernel(
    mine_ref, peer_ref, raw_ref, alpha_ref, near_ref, tail_ref, before_ref, after_ref, wcat_ref, ends_ref, bias_ref, audio_ref,
    out_ref, act_ref, y_ref, out_top_ref, out_low_ref, top_sem, low_sem,
):
    del audio_ref
    core, chip = lax.axis_index("c"), lax.axis_index("zh")
    owners, slots, half = mine_ref.shape
    count = out_ref.shape[0]
    places = owners * slots
    first = core == 0
    mine = mine_ref[...].astype(F32).reshape(places, half)
    peer = peer_ref[...].astype(F32).reshape(places, half)
    left = jnp.where(first, mine, peer).astype(BF16)
    right = jnp.where(first, peer, mine).astype(BF16)
    row = iota((HEAD + EDGE, places), 0)
    place = iota((HEAD + EDGE, places), 1)
    own_place = (row // CAP) * slots + row % CAP
    after = row - HEAD
    after_place = (after // CAP) * slots + CAP + after % CAP
    pick = (place == jnp.where(row < HEAD, own_place, after_place)).astype(F32).astype(BF16)
    alpha = alpha_ref[0:1]
    inv = 1.0 / alpha
    taken = []
    for k, side in ((0, left), (1, right)):
        cols = slice(k * half, (k + 1) * half)
        got = jnp.dot(pick, side, preferred_element_type=F32)
        taken.append(got[:HEAD])
        mix = raw_ref[:, cols].astype(F32) + got[:HEAD]
        act_ref[EDGE : EDGE + HEAD, cols] = (mix + sin_squared(alpha[:, cols] * mix) * inv[:, cols]).astype(BF16)
        mix = after_ref[:, cols].astype(F32) + got[HEAD:]
        act_ref[EDGE + HEAD + 4 * EDGE :, cols] = (mix + sin_squared(alpha[:, cols] * mix) * inv[:, cols]).astype(BF16)
    act_ref[0:EDGE] = before_ref[EDGE:]
    act_ref[EDGE + HEAD : EDGE + HEAD + 2 * EDGE] = near_ref[...]
    act_ref[EDGE + HEAD + 2 * EDGE : EDGE + HEAD + 4 * EDGE] = tail_ref[...]
    y_ref[...] = jnp.dot(act_ref[...], wcat_ref[...], preferred_element_type=F32)
    bias = bias_ref[...]
    width = bias.shape[1]
    got = taken[0][:, 0:width]
    for k in range(1, 2 * half // width):
        at = k * width % half
        got = jnp.where(chip * 2 + core == k, taken[k * width // half][:, at : at + width], got)
    conv = taps_sum(y_ref, EDGE, TOP)
    mix = ends_ref[0:TOP].astype(F32)
    out_top_ref[0:HEAD] = (mix[:HEAD] + got + bias + conv[:HEAD]).astype(BF16)
    out_top_ref[HEAD:] = (mix[HEAD:] + bias + conv[HEAD:]).astype(BF16)
    conv = taps_sum(y_ref, EDGE + HEAD + 3 * EDGE, EDGE)
    out_low_ref[...] = (ends_ref[TOP:].astype(F32) + bias + conv).astype(BF16)
    top_copy = pltpu.make_async_copy(out_top_ref, out_ref.at[0:TOP], top_sem)
    low_copy = pltpu.make_async_copy(out_low_ref, out_ref.at[count - EDGE : count], low_sem)
    top_copy.start()
    low_copy.start()
    top_copy.wait()
    low_copy.wait()


def final_conv(mine, peer, raw, alpha, near, tail, before, after, wcat, ends, bias, audio):
    count, width = audio.shape
    channels = raw.shape[1]
    stack = EDGE + HEAD + 5 * EDGE
    return call(
        final_kernel,
        "final_conv",
        pltpu.HBM((count, width), BF16),
        (mine, peer, raw, alpha, near, tail, before, after, wcat, ends, bias, audio),
        scratch=[
            pltpu.VMEM((stack, channels), BF16),
            pltpu.VMEM((stack, TAPS * width), F32),
            pltpu.VMEM((TOP, width), BF16),
            pltpu.VMEM((EDGE, width), BF16),
            DMA,
            DMA,
        ],
        far=(11,),
        far_outs=(0,),
        mib=16,
        alias={11: 0},
        cost=work(3),
    )


def rotate(x, d):
    return lax.ppermute(x, "zh", [(i, (i + d) % ZH) for i in range(ZH)])


def swap(x):
    return lax.ppermute(x, "c", [(0, 1), (1, 0)])


def after_all(x, *tokens):
    return lax.optimization_barrier((x, *tokens))[0]


def body(
    query, new_key, new_value, cache_key, cache_value, cache_len, residual, out_weight, norm_gain, codec_weight,
    finished, owner, frames, snake_alpha, filter_weight, conv_bias,
):
    owners = lax.axis_size("dp")
    width = norm_gain.shape[0]

    sent = payload(frames, snake_alpha)
    left, right = rotate(sent, 1), rotate(sent, 3)
    query = after_all(query, sent)
    theirs, attended, weight, targets = attend(
        query, new_key, new_value, cache_key, cache_value, cache_len, finished, owner, out_weight, width
    )
    peer = swap(theirs)
    own, codec, gain = project(attended, weight, residual, codec_weight, norm_gain)
    got = {d: rotate(x, d) for d, x in zip(ORDER, pair(own, peer))}
    hidden, keep, send = hidden_step(own, peer, got[2], got[1], got[3], gain, codec)

    far_head = rotate(after_all(left[:CUT], hidden), 1)
    far_rest = rotate(after_all(right[CUT:], hidden), 3)
    pieces = []
    for x in (sent, right, far_head, far_rest, left):
        pieces += [x, swap(x)]

    joined = join(keep, swap(send))
    parts = [joined] + [rotate(joined, d) for d in (2, 1, 3)]
    audio, raw, alpha, close, tail, wcat, ends, bias = main_conv(pieces, filter_weight, frames, conv_bias)
    before = lax.ppermute(tail, "dp", [(i, i + 1) for i in range(owners - 1)])
    after = lax.ppermute(raw[:EDGE], "dp", [(i + 1, i) for i in range(owners - 1)])
    targets = after_all(targets, tail)
    outgoing = dispatch(residual.shape[1], owners, parts, targets)
    incoming = lax.all_to_all(outgoing, "dp", 0, 0, tiled=True)
    other = swap(incoming)
    audio = final_conv(incoming, other, raw, alpha, close, tail, before, after, wcat, ends, bias, audio)
    return (hidden, audio)


def solution(mesh):
    torus = Mesh(mesh.devices.reshape(mesh.shape["dp"], ZH, 2), ("dp", "zh", "c"))
    return jax.shard_map(
        body,
        mesh=torus,
        in_specs=(
            P("dp", MP), P("dp", MP), P("dp", MP), P("dp", MP, None, None), P("dp", MP, None, None), P("dp"), P("dp", None),
            P(MP, None), P(MP), P(MP, None), P("dp"), P("dp"), P("dp", MP), P(MP), P(None, None, MP), P(MP),
        ),
        out_specs=(P("dp", MP), P("dp", MP)),
        check_vma=False,
    )
```

```python
import math
import jax
import jax.numpy as jnp
from jax import lax
from jax.experimental import pallas as pl
from jax.experimental.pallas import tpu as pltpu
from jax.sharding import Mesh
from jax.sharding import PartitionSpec as P

TAPS = 7
STEP = 3
CAP = 4
ZH = 4
MP = ("zh", "c")
F32 = jnp.float32
BF16 = jnp.bfloat16
ORDER = (2, 1, 3, 0)
HEAD = 32 * CAP
EDGE = 16
TOP = HEAD + EDGE
VM = pl.BlockSpec(memory_space=pltpu.VMEM)
ANY = pl.BlockSpec(memory_space=pl.ANY)
DMA = pltpu.SemaphoreType.DMA


def params(mib=8):
    return pltpu.CompilerParams(vmem_limit_bytes=mib * 1024 * 1024)


def sds(shape, dtype):
    return jax.ShapeDtypeStruct(shape, dtype)


def placed_in(x, space):
    return pltpu.with_memory_space_constraint(x, space)


def call(kernel, name, outs, ins, scratch=(), far=(), far_outs=(), mib=8, alias=None, cost=None):
    return pl.pallas_call(
        kernel,
        in_specs=[ANY if i in far else VM for i in range(len(ins))],
        out_specs=[ANY if i in far_outs else VM for i in range(len(outs))] if isinstance(outs, list) else ANY if far_outs else VM,
        out_shape=outs,
        scratch_shapes=list(scratch),
        input_output_aliases=alias or {},
        compiler_params=params(mib),
        cost_estimate=cost,
        name=name,
    )(*[placed_in(x, pltpu.HBM if i in far else pltpu.VMEM) for i, x in enumerate(ins)])


def work(us):
    return pl.CostEstimate(flops=int(us * 1e7), transcendentals=0, bytes_accessed=int(us * 3e4))


def iota(shape, dim):
    return lax.broadcasted_iota(jnp.int32, shape, dim)


def as_column(row, size):
    diag = iota((size, size), 0) == iota((size, size), 1)
    return jnp.sum(jnp.where(diag, jnp.broadcast_to(row, (size, size)), 0), axis=1, keepdims=True)


def sin_squared(x):
    k = jnp.floor(x * (1.0 / math.pi) + 0.5)
    r = x - k * 3.140625
    r = r - k * 9.67502593994140625e-4
    r = r - k * 1.509957990978376432e-7
    s = r * r
    p = -1.0 / 39916800.0
    p = p * s + 1.0 / 362880.0
    p = p * s - 1.0 / 5040.0
    p = p * s + 1.0 / 120.0
    p = p * s - 1.0 / 6.0
    y = r + r * (s * p)
    return y * y


def attend_kernel(
    q_hbm, nk_hbm, nv_hbm, ck_hbm, cv_hbm, len_hbm, fin_hbm, own_hbm, w_hbm,
    theirs_ref, att_ref, weight_ref, tgt_ref,
    q_ref, nk_ref, nv_ref, ck_ref, cv_ref, len_ref, fin_ref, own_ref, peer_ref, small_sem, key_sem, value_sem, peer_sem, own_sem,
):
    rows, heads, places, depth = ck_ref.shape
    group = 16
    groups = rows // group
    wide = group * places
    width = weight_ref.shape[2]
    chip, core = lax.axis_index("zh"), lax.axis_index("c")
    small = [
        pltpu.make_async_copy(src, dst, small_sem.at[i])
        for i, (src, dst) in enumerate(
            [(q_hbm, q_ref), (nk_hbm, nk_ref), (nv_hbm, nv_ref), (len_hbm, len_ref), (fin_hbm, fin_ref), (own_hbm, own_ref)]
        )
    ]
    keys, values, theirs, ours = [], [], [], []
    for g in range(groups):
        span = pl.ds(g * group, group)
        keys.append(pltpu.make_async_copy(ck_hbm.at[span], ck_ref.at[span], key_sem.at[g]))
        values.append(pltpu.make_async_copy(cv_hbm.at[span], cv_ref.at[span], value_sem.at[g]))
    for i, d in enumerate(ORDER):
        block = lax.rem(chip + d, ZH) * 2
        for held, to, sem, side in ((theirs, peer_ref, peer_sem, 1 - core), (ours, weight_ref, own_sem, core)):
            at = pl.multiple_of((block + side) * width, width)
            held.append(pltpu.make_async_copy(w_hbm.at[:, pl.ds(at, width)], to.at[i], sem.at[i]))
    for copy in small:
        copy.start()
    for g in range(groups):
        keys[g].start()
        values[g].start()
    for copy in theirs + ours:
        copy.start()
    for copy in small:
        copy.wait()
    scale = 1.0 / math.sqrt(depth)

    fin = fin_ref[...]
    owner = own_ref[...]
    fin_col = as_column(fin, rows)
    owner_col = as_column(owner, rows)
    earlier = (owner_col == owner) & (fin_col == 1) & (iota((rows, rows), 0) < iota((rows, rows), 1))
    slot = jnp.sum(earlier.astype(jnp.int32), axis=0, keepdims=True)
    done = fin == 1
    tgt_ref[0:1] = jnp.where(done, owner * (2 * CAP) + slot, -1)
    tgt_ref[1:2] = jnp.where(done & (owner >= 1), (owner - 1) * (2 * CAP) + CAP + slot, -1)

    length = as_column(len_ref[...], rows)
    offset = iota((group, wide), 1) - places * iota((group, wide), 0)
    for g in range(groups):
        span = slice(g * group, (g + 1) * group)
        inside = (offset >= 0) & (offset < length[span])
        valid = jnp.concatenate([inside.astype(F32)] * heads, axis=0) > 0.5
        keys[g].wait()
        scores, own = [], []
        for h in range(heads):
            cols = slice(h * depth, (h + 1) * depth)
            q = q_ref[span, cols]
            k = ck_ref[span, h].reshape(wide, depth)
            scores.append(lax.dot_general(q, k, (((1,), (1,)), ((), ())), preferred_element_type=F32))
            own.append(jnp.sum(q.astype(F32) * nk_ref[span, cols].astype(F32), axis=1, keepdims=True))
        scores = jnp.where(valid, jnp.concatenate(scores, axis=0) * scale, -1e30)
        own = jnp.concatenate(own, axis=0) * scale
        top = jnp.maximum(jnp.max(scores, axis=1, keepdims=True), own)
        expo = jnp.where(valid, jnp.exp(scores - top), 0.0)
        own_expo = jnp.exp(own - top)
        inv = 1.0 / (jnp.sum(expo, axis=1, keepdims=True) + own_expo)
        weights = (expo * inv).astype(BF16)
        own_weight = (own_expo * inv).astype(BF16).astype(F32)
        values[g].wait()
        for h in range(heads):
            cols = slice(h * depth, (h + 1) * depth)
            part = slice(h * group, (h + 1) * group)
            mixed = jnp.dot(weights[part], cv_ref[span, h].reshape(wide, depth), preferred_element_type=F32)
            att_ref[span, cols] = (mixed + own_weight[part] * nv_ref[span, cols].astype(F32)).astype(BF16)
    att = att_ref[...]
    for i in range(ZH):
        theirs[i].wait()
        theirs_ref[i] = jnp.dot(att, peer_ref[i], preferred_element_type=F32).astype(BF16)
    for copy in ours:
        copy.wait()


def attend(query, new_key, new_value, cache_key, cache_value, cache_len, finished, owner, weight, width):
    rows = query.shape[0]
    depth = weight.shape[0]
    line = lambda x: x.reshape(1, rows)
    ins = (query, new_key, new_value, cache_key, cache_value, line(cache_len), line(finished), line(owner), weight)
    dma = DMA
    return call(
        attend_kernel,
        "attend",
        [
            pltpu.VMEM((ZH, rows, width), BF16),
            pltpu.VMEM((rows, depth), BF16),
            pltpu.VMEM((ZH, depth, width), BF16),
            pltpu.VMEM((2, rows), jnp.int32),
        ],
        ins,
        scratch=[pltpu.VMEM(x.shape, x.dtype) for x in ins[:8]]
        + [pltpu.VMEM((ZH, depth, width), BF16), dma((6,)), dma((rows // 16,)), dma((rows // 16,)), dma((ZH,)), dma((ZH,))],
        far=range(9),
        mib=16,
        cost=work(6),
    )


def project_kernel(att_ref, w_ref, res_hbm, codec_hbm, gain_hbm, out_ref, codec_ref, gain_ref, res_ref, line_ref, sems):
    width = w_ref.shape[2]
    at = pl.multiple_of((lax.axis_index("zh") * 2 + lax.axis_index("c")) * width, width)
    res_copy = pltpu.make_async_copy(res_hbm.at[:, pl.ds(at, width)], res_ref, sems.at[0])
    gain_copy = pltpu.make_async_copy(gain_hbm, line_ref, sems.at[1])
    codec_copy = pltpu.make_async_copy(codec_hbm, codec_ref, sems.at[2])
    res_copy.start()
    gain_copy.start()
    codec_copy.start()
    att = att_ref[...]
    for i, d in enumerate(ORDER):
        part = jnp.dot(att, w_ref[i], preferred_element_type=F32)
        if d == 0:
            res_copy.wait()
            part = part + res_ref[...].astype(F32)
        out_ref[i] = part
    gain_copy.wait()
    gain_ref[...] = line_ref[...].astype(F32).reshape(1, width)
    codec_copy.wait()


def project(attended, weight, residual, codec, gain):
    rows = attended.shape[0]
    count, _, width = weight.shape
    return call(
        project_kernel,
        "project",
        [pltpu.VMEM((count, rows, width), F32), pltpu.VMEM(codec.shape, BF16), pltpu.VMEM((1, width), F32)],
        (attended, weight, residual, codec, gain),
        scratch=[pltpu.VMEM((rows, width), BF16), pltpu.VMEM(gain.shape, BF16), DMA((3,))],
        far=(2, 3, 4),
        cost=work(2),
    )


def pair_kernel(own_ref, peer_ref, *outs):
    for i, out in enumerate(outs):
        out[...] = (own_ref[i] + peer_ref[i].astype(F32)).astype(BF16)


def pair(own, peer):
    _, rows, width = own.shape
    return call(pair_kernel, "pair", [pltpu.VMEM((rows, width), BF16)] * (ZH - 1), (own, peer), cost=work(0.5))


def squares_row(total):
    rows = total.shape[0]
    diag = iota((rows, 128), 0) == iota((rows, 128), 1)
    line = jnp.sum(jnp.where(diag, jnp.broadcast_to(total, (rows, 128)), 0.0), axis=0, keepdims=True)
    hi = line.astype(BF16).astype(F32)
    return hi, line - hi


def squares_column(line, rows):
    diag = iota((rows, 128), 0) == iota((rows, 128), 1)
    return jnp.sum(jnp.where(diag, jnp.broadcast_to(line, (rows, 128)), 0.0), axis=1, keepdims=True)


def with_squares(block, hi, lo):
    row = iota(block.shape, 0)
    return jnp.where(row == 0, hi, jnp.where(row == 1, lo, block))


def hidden_kernel(
    own_ref, peer_ref, r2_ref, r1_ref, r3_ref, gain_ref, codec_ref, before_ref, after_ref, hid_hbm, keep_ref, send_ref, total_ref, hid_ref, sem
):
    half = codec_ref.shape[1] // 2
    width = codec_ref.shape[0]
    last = ORDER.index(0)
    total = own_ref[last] + peer_ref[last].astype(F32)
    total = total + r2_ref[...].astype(F32) + (r1_ref[...].astype(F32) + r3_ref[...].astype(F32))
    hidden = total.astype(BF16)
    hid_ref[...] = hidden
    copy = pltpu.make_async_copy(hid_ref, hid_hbm, sem)
    copy.start()
    wide = hidden.astype(F32)
    normed = (wide * gain_ref[...]).astype(BF16)
    squares = jnp.sum(wide * wide, axis=1, keepdims=True)
    part = jnp.dot(normed, codec_ref[...], preferred_element_type=F32)
    left, right = part[:, :half], part[:, half:]
    first = lax.axis_index("c") == 0
    keep_ref[...] = jnp.where(first, left, right)
    send_ref[:, :half] = jnp.where(first, right, left).astype(BF16)
    total_ref[...] = squares
    hi, lo = squares_row(squares)
    send_ref[0:EDGE, half:] = with_squares(before_ref[...].astype(F32), hi, lo).astype(BF16)
    send_ref[EDGE : 2 * EDGE, half:] = after_ref[...]
    send_ref[2 * EDGE :, half:] = jnp.zeros((send_ref.shape[0] - 2 * EDGE, 128), BF16)
    copy.wait()


def hidden_step(own, peer, r2, r1, r3, gain, codec, before, after):
    rows, width = r2.shape
    half = codec.shape[1] // 2
    outs = [
        pltpu.HBM((rows, width), BF16),
        pltpu.VMEM((rows, half), F32),
        pltpu.VMEM((rows, half + 128), BF16),
        pltpu.VMEM((rows, 1), F32),
    ]
    ins = (own, peer, r2, r1, r3, gain, codec, before, after)
    return call(hidden_kernel, "hidden", outs, ins, [pltpu.VMEM((rows, width), BF16), DMA], far_outs=(0,), cost=work(2))


def join_kernel(keep_ref, total_ref, recv_ref, before_ref, after_ref, out_ref):
    half = keep_ref.shape[1]
    first = lax.axis_index("c") == 0
    out_ref[:, :half] = (keep_ref[...] + recv_ref[:, :half].astype(F32)).astype(BF16)
    mate = recv_ref[:, half:].astype(F32)
    line = mate[0:1] + mate[1:2]
    mine_hi, mine_lo = squares_row(total_ref[...])
    line = line + (mine_hi + mine_lo)
    hi = line.astype(BF16).astype(F32)
    for at, own, other in ((0, before_ref, mate[0:EDGE]), (2 * EDGE, after_ref, mate[EDGE : 2 * EDGE])):
        own = own[...].astype(F32)
        low = jnp.where(first, own, other)
        if at == 0:
            low = with_squares(low, hi, line - hi)
        out_ref[at : at + EDGE, half:] = low.astype(BF16)
        out_ref[at + EDGE : at + 2 * EDGE, half:] = jnp.where(first, other, own).astype(BF16)


def join(keep, total, recv, before, after):
    return call(join_kernel, "join", pltpu.VMEM(recv.shape, BF16), (keep, total, recv, before, after), cost=work(0.3))


def dispatch_kernel(features, a_ref, b_ref, c_ref, d_ref, tgt_ref, out_ref):
    half = a_ref.shape[1] - 128
    owners, slots, _ = out_ref.shape
    rows = a_ref.shape[0]
    parts = (a_ref, b_ref, c_ref, d_ref)
    a, b, c, d = (p[:, :half].astype(F32) for p in parts)
    a2, b2, c2, d2 = (p[0:EDGE, half:].astype(F32) for p in parts)
    total = (a + b) + (c + d)
    lines = (a2 + b2) + (c2 + d2)
    squares = squares_column(lines[0:1] + lines[1:2], rows)
    latent = (total * lax.rsqrt(squares / features + 1e-05)).astype(BF16)
    place = iota((owners * slots, rows), 0)
    onehot = ((place == tgt_ref[0:1]) | (place == tgt_ref[1:2])).astype(F32).astype(BF16)
    placed = jnp.dot(onehot, latent, preferred_element_type=F32)
    out_ref[...] = placed.reshape(owners, slots, half).astype(BF16)


def dispatch(features, owners, parts, targets):
    half = parts[0].shape[1] - 128
    kernel = lambda *refs: dispatch_kernel(features, *refs)
    return call(kernel, "dispatch", pltpu.VMEM((owners, 2 * CAP, half), BF16), (*parts, targets), cost=work(1))


def payload_kernel(
    frames_hbm, alpha_hbm, filt_hbm, bias_hbm, out_ref, head_ref, tail_ref, frames_ref, wcat_ref, bias_ref, alpha_ref, sems
):
    copies = [
        pltpu.make_async_copy(alpha_hbm, alpha_ref, sems.at[0]),
        pltpu.make_async_copy(frames_hbm, frames_ref, sems.at[1]),
        pltpu.make_async_copy(bias_hbm, bias_ref, sems.at[2]),
    ]
    width = frames_ref.shape[1]
    for t in range(TAPS):
        copies.append(pltpu.make_async_copy(filt_hbm.at[t], wcat_ref.at[:, pl.ds(t * width, width)], sems.at[3 + t]))
    for copy in copies:
        copy.start()
    for copy in copies[:2]:
        copy.wait()
    count = frames_ref.shape[0]
    first = out_ref.shape[0] - count
    raw = frames_ref[...]
    alpha = alpha_ref[...]
    mix = raw[HEAD:].astype(F32)
    act = mix + sin_squared(alpha * mix) * (1.0 / alpha)
    out_ref[0:HEAD] = raw[:HEAD]
    out_ref[HEAD:count] = act.astype(BF16)
    head_ref[...] = raw[:EDGE]
    tail_ref[...] = act[count - HEAD - EDGE :].astype(BF16)
    hi = alpha.astype(BF16).astype(F32)
    mid = (alpha - hi).astype(BF16).astype(F32)
    lo = alpha - hi - mid
    row = iota((first, width), 0)
    out_ref[count:] = jnp.where(row == 0, hi, jnp.where(row == 1, mid, jnp.where(row == 2, lo, 0.0))).astype(BF16)
    for copy in copies[2:]:
        copy.wait()


def payload(frames, alpha, filt, bias):
    count, width = frames.shape
    channels = filt.shape[1]
    return call(
        payload_kernel,
        "payload",
        [
            pltpu.VMEM((count + 16, width), BF16),
            pltpu.VMEM((EDGE, width), BF16),
            pltpu.VMEM((EDGE, width), BF16),
            pltpu.VMEM((count, width), BF16),
            pltpu.VMEM((channels, TAPS * width), BF16),
            pltpu.VMEM((1, width), F32),
        ],
        (frames, alpha.reshape(1, width), filt, bias.reshape(1, width)),
        scratch=[pltpu.VMEM((1, width), F32), DMA((3 + TAPS,))],
        far=(0, 1, 2, 3),
        cost=work(2),
    )


def taps_sum(y, base, count):
    total = None
    for t in range(TAPS):
        at = base + (t - TAPS // 2) * STEP
        part = y[at : at + count, t * 128 : (t + 1) * 128]
        total = part if total is None else total + part
    return total


def main_kernel(*refs):
    pieces = refs[:8]
    wcat_ref, own_ref, bias_ref, audio_hbm, raw_ref, alpha_ref, near_ref, tail_ref = refs[8:16]
    act_ref, y_ref, out_ref, sem = refs[16:]
    chip, core = lax.axis_index("zh"), lax.axis_index("c")
    count = own_ref.shape[0]
    for k in range(8):
        source = lax.rem(chip + k // 2, ZH) * 2 + (core if k % 2 == 0 else 1 - core)
        cols = pl.ds(pl.multiple_of(source * 128, 128), 128)
        head = pieces[k]
        act_ref[:, cols] = head[HEAD:count]
        raw_ref[:, cols] = head[0:HEAD]
        extra = head[count : count + 16].astype(F32)
        alpha_ref[:, cols] = jnp.broadcast_to(extra[0:1] + extra[1:2] + extra[2:3], (8, 128))
    near_ref[...] = act_ref[0 : 2 * EDGE]
    tail_ref[...] = act_ref[count - HEAD - 2 * EDGE : count - HEAD]
    y_ref[...] = jnp.dot(act_ref[...], wcat_ref[...], preferred_element_type=F32)
    inner = count - TOP - EDGE
    conv = taps_sum(y_ref, EDGE, inner)
    mix = own_ref[TOP : TOP + inner].astype(F32)
    out_ref[...] = (mix + bias_ref[...] + conv).astype(BF16)
    last = pltpu.make_async_copy(out_ref, audio_hbm.at[pl.ds(TOP, inner)], sem)
    last.start()
    last.wait()


def main_conv(pieces, wcat, own, bias):
    count, width = own.shape
    channels = wcat.shape[0]
    outs = [
        pltpu.HBM((count, width), BF16),
        pltpu.VMEM((HEAD, channels), BF16),
        pltpu.VMEM((8, channels), F32),
        pltpu.VMEM((2 * EDGE, channels), BF16),
        pltpu.VMEM((2 * EDGE, channels), BF16),
    ]
    scratch = [
        pltpu.VMEM((count - HEAD, channels), BF16),
        pltpu.VMEM((count - HEAD, TAPS * width), F32),
        pltpu.VMEM((count - TOP - EDGE, width), BF16),
        DMA,
    ]
    return call(main_kernel, "main_conv", outs, (*pieces, wcat, own, bias), scratch, far_outs=(0,), mib=16, cost=work(4))


def final_kernel(
    mine_ref, peer_ref, raw_ref, alpha_ref, near_ref, tail_ref, p0_ref, p1_ref, p2_ref, p3_ref, wcat_ref, ends_ref, bias_ref, audio_ref,
    out_ref, act_ref, after_ref, y_ref, out_top_ref, out_low_ref, top_sem, low_sem,
):
    del audio_ref
    core, chip = lax.axis_index("c"), lax.axis_index("zh")
    owners, slots, half = mine_ref.shape
    count = out_ref.shape[0]
    places = owners * slots
    first = core == 0
    mine = mine_ref[...].astype(F32).reshape(places, half)
    peer = peer_ref[...].astype(F32).reshape(places, half)
    left = jnp.where(first, mine, peer).astype(BF16)
    right = jnp.where(first, peer, mine).astype(BF16)
    row = iota((HEAD + EDGE, places), 0)
    place = iota((HEAD + EDGE, places), 1)
    own_place = (row // CAP) * slots + row % CAP
    after = row - HEAD
    after_place = (after // CAP) * slots + CAP + after % CAP
    pick = (place == jnp.where(row < HEAD, own_place, after_place)).astype(F32).astype(BF16)
    alpha = alpha_ref[0:1]
    inv = 1.0 / alpha
    for d, part in enumerate((p0_ref, p1_ref, p2_ref, p3_ref)):
        for k in range(2):
            cols = pl.ds(pl.multiple_of((lax.rem(chip + ZH - d, ZH) * 2 + k) * 128, 128), 128)
            act_ref[0:EDGE, cols] = part[k * EDGE : (k + 1) * EDGE, half:]
            after_ref[:, cols] = part[(2 + k) * EDGE : (3 + k) * EDGE, half:]
    taken = []
    for k, side in ((0, left), (1, right)):
        cols = slice(k * half, (k + 1) * half)
        got = jnp.dot(pick, side, preferred_element_type=F32)
        taken.append(got[:HEAD])
        mix = raw_ref[:, cols].astype(F32) + got[:HEAD]
        act_ref[EDGE : EDGE + HEAD, cols] = (mix + sin_squared(alpha[:, cols] * mix) * inv[:, cols]).astype(BF16)
        mix = after_ref[:, cols].astype(F32) + got[HEAD:]
        act_ref[EDGE + HEAD + 4 * EDGE :, cols] = (mix + sin_squared(alpha[:, cols] * mix) * inv[:, cols]).astype(BF16)
    act_ref[EDGE + HEAD : EDGE + HEAD + 2 * EDGE] = near_ref[...]
    act_ref[EDGE + HEAD + 2 * EDGE : EDGE + HEAD + 4 * EDGE] = tail_ref[...]
    y_ref[...] = jnp.dot(act_ref[...], wcat_ref[...], preferred_element_type=F32)
    bias = bias_ref[...]
    width = bias.shape[1]
    got = taken[0][:, 0:width]
    for k in range(1, 2 * half // width):
        at = k * width % half
        got = jnp.where(chip * 2 + core == k, taken[k * width // half][:, at : at + width], got)
    conv = taps_sum(y_ref, EDGE, TOP)
    mix = ends_ref[0:TOP].astype(F32)
    out_top_ref[0:HEAD] = (mix[:HEAD] + got + bias + conv[:HEAD]).astype(BF16)
    out_top_ref[HEAD:] = (mix[HEAD:] + bias + conv[HEAD:]).astype(BF16)
    conv = taps_sum(y_ref, EDGE + HEAD + 3 * EDGE, EDGE)
    out_low_ref[...] = (ends_ref[count - EDGE : count].astype(F32) + bias + conv).astype(BF16)
    top_copy = pltpu.make_async_copy(out_top_ref, out_ref.at[0:TOP], top_sem)
    low_copy = pltpu.make_async_copy(out_low_ref, out_ref.at[count - EDGE : count], low_sem)
    top_copy.start()
    low_copy.start()
    top_copy.wait()
    low_copy.wait()


def final_conv(mine, peer, raw, alpha, near, tail, parts, wcat, ends, bias, audio):
    count, width = audio.shape
    channels = raw.shape[1]
    stack = EDGE + HEAD + 5 * EDGE
    return call(
        final_kernel,
        "final_conv",
        pltpu.HBM((count, width), BF16),
        (mine, peer, raw, alpha, near, tail, *parts, wcat, ends, bias, audio),
        scratch=[
            pltpu.VMEM((stack, channels), BF16),
            pltpu.VMEM((EDGE, channels), BF16),
            pltpu.VMEM((stack, TAPS * width), F32),
            pltpu.VMEM((TOP, width), BF16),
            pltpu.VMEM((EDGE, width), BF16),
            DMA,
            DMA,
        ],
        far=(13,),
        far_outs=(0,),
        mib=16,
        alias={13: 0},
        cost=work(3),
    )


def rotate(x, d):
    return lax.ppermute(x, "zh", [(i, (i + d) % ZH) for i in range(ZH)])


def swap(x):
    return lax.ppermute(x, "c", [(0, 1), (1, 0)])


def after_all(x, *tokens):
    return lax.optimization_barrier((x, *tokens))[0]


def body(
    query, new_key, new_value, cache_key, cache_value, cache_len, residual, out_weight, norm_gain, codec_weight,
    finished, owner, frames, snake_alpha, filter_weight, conv_bias,
):
    owners = lax.axis_size("dp")
    width = norm_gain.shape[0]

    sent, head, tail, mine, wcat, bias = payload(frames, snake_alpha, filter_weight, conv_bias)
    left = rotate(sent, 1)
    right = rotate(sent, 3)
    before = lax.ppermute(tail, "dp", [(i, i + 1) for i in range(owners - 1)])
    after = lax.ppermute(head, "dp", [(i + 1, i) for i in range(owners - 1)])
    query = after_all(query, sent)
    theirs, attended, weight, targets = attend(
        query, new_key, new_value, cache_key, cache_value, cache_len, finished, owner, out_weight, width
    )
    theirs = after_all(theirs, left, right, before, after)
    peer = swap(theirs)
    own, codec, gain = project(attended, weight, residual, codec_weight, norm_gain)
    pairs = pair(own, peer)
    got = {d: rotate(x, d) for d, x in zip(ORDER, pairs)}
    far = rotate(after_all(right, pairs[0]), 3)
    hidden, keep, send, total = hidden_step(own, peer, got[2], got[1], got[3], gain, codec, before, after)
    joined = join(keep, total, swap(send), before, after)
    parts = [joined] + [rotate(joined, d) for d in (1, 2, 3)]
    pieces = []
    for x, when in ((sent, joined), (right, joined), (far, parts[1]), (left, joined)):
        pieces += [x, swap(after_all(x, when))]
    audio, raw, alpha, close, low = main_conv(pieces, wcat, mine, bias)
    targets = after_all(targets, low)
    outgoing = dispatch(residual.shape[1], owners, parts, targets)
    incoming = lax.all_to_all(outgoing, "dp", 0, 0, tiled=True)
    other = swap(incoming)
    audio = final_conv(incoming, other, raw, alpha, close, low, parts, wcat, mine, bias, audio)
    return (hidden, audio)


def solution(mesh):
    torus = Mesh(mesh.devices.reshape(mesh.shape["dp"], ZH, 2), ("dp", "zh", "c"))
    return jax.shard_map(
        body,
        mesh=torus,
        in_specs=(
            P("dp", MP), P("dp", MP), P("dp", MP), P("dp", MP, None, None), P("dp", MP, None, None), P("dp"), P("dp", None),
            P(MP, None), P(MP), P(MP, None), P("dp"), P("dp"), P("dp", MP), P(MP), P(None, None, MP), P(MP),
        ),
        out_specs=(P("dp", MP), P("dp", MP)),
        check_vma=False,
    )
```
